512 devices in a mesh: leaf: 32 (over z, core), region: 16 (over x, y).
Axes of the slice: x: 4, y: 4, z: 16, core: 2. Of those that a mesh axis runs over, the one named last changes fastest.
Arguments:
- leaf_factor: bfloat16 [16, 32768, 1024], P('region', 'leaf'), as said below
- basis_pool: bfloat16 [16, 32768, 512], P('region', 'leaf'), may hold values from -6 to 6
- root_basis: bfloat16 [16, 32768, 256], P('region', 'leaf'), may hold values from -6 to 6
- responses: bfloat16 [16, 32768, 256], P('region', 'leaf'), may hold values from -48 to 48
- knot_order: int32 [16, 512], P('region'), may hold values from 0 to 511, each once within a row
- region_prior: bfloat16 [16, 256, 256], P('region'), as said below
- root_prior: bfloat16 [256, 256], replicated, as said below
Outputs:
- predictions: bfloat16 [16, 32768, 256], P('region', 'leaf')
- region_factor: float32 [16, 256, 256], P('region', 'leaf')
- root_factor: float32 [256, 256], P('leaf')
The draws below stay inside these ranges and needn't reach their ends.
Inputs may be any that keep to these rules, and one draw needn't show every extreme that they name: `knot_order`: each row lists every candidate column exactly once. `leaf_factor`: each leaf block has a diagonal near one that dominates its other entries. `region_prior`: symmetric and positive definite. `root_prior`: symmetric and positive definite.
All inputs are finite; a program needn't handle non-finite values.
Results may differ from the reference program's by a relative error of at most 0.0038.
Values sent between devices are 32-bit elements; how exact they have to be, the bound alone decides.
No kernel may reach another device: no remote copies, remote signals or barrier semaphores. Data moves between devices by JAX's collectives and lax.ppermute only.
A program may use at most 64 MiB of HBM per device.

```python
import math
import jax
import jax.numpy as jnp
from jax import lax

LEAF = 1024
K = 256
K0 = 256
R = 256
POOL = 512
REGIONS = 16
OBS_REG = 32768
N_LEAF = 32
N_REGION = 16


lag_decay = 0.8


lag_taps = 12


def draw_leaf_factor(key, part):
    noise = jax.random.normal(key, (REGIONS, OBS_REG, LEAF), jnp.float32) * 0.5
    noise = noise / jnp.sqrt(jnp.float32(LEAF))
    row_ids = jnp.arange(OBS_REG)[:, None] % LEAF
    col_ids = jnp.arange(LEAF)[None, :]
    unit = (row_ids == col_ids).astype(jnp.float32)
    return (unit[None] + noise).astype(jnp.bfloat16)


def unit_noise(key, shape):
    values = jax.random.normal(key, shape, jnp.float32)
    return values


def smooth_noise(key, array_shape):
    column_count = array_shape[-1]
    raw_noise = unit_noise(key, tuple(array_shape[:-1]) + (column_count + lag_taps - 1,))
    scale_total = math.sqrt(sum((lag_decay ** (2 * offset) for offset in range(lag_taps))))
    smoothed = jnp.zeros(array_shape, jnp.float32)
    for offset in range(lag_taps):
        smoothed = smoothed + lag_decay ** offset / scale_total * raw_noise[..., offset:offset + column_count]
    return smoothed


def shared_pool(key):
    values = smooth_noise(jax.random.fold_in(key, 11), (REGIONS, OBS_REG, POOL))
    return jnp.clip(values, -6.0, 6.0)


def root_from_pool(key, pool):
    mixing = jax.random.normal(jax.random.fold_in(key, 13), (POOL, K0), jnp.float32) / jnp.sqrt(jnp.float32(POOL))
    mixed = jnp.einsum('roc,ck->rok', pool, mixing)
    extra = smooth_noise(jax.random.fold_in(key, 17), (REGIONS, OBS_REG, K0))
    return jnp.clip(0.5 * mixed + 0.866 * extra, -6.0, 6.0)


def draw_basis_pool(key, part):
    return shared_pool(key).astype(jnp.bfloat16)


def draw_root_basis(key, part):
    return root_from_pool(key, shared_pool(key)).astype(jnp.bfloat16)


def draw_responses(key, part):
    root_vals = root_from_pool(key, shared_pool(key))
    weights = jax.random.normal(jax.random.fold_in(key, 19), (K0, R), jnp.float32) * (4.0 / jnp.sqrt(jnp.float32(K0)))
    signal = jnp.einsum('rok,kc->roc', root_vals, weights)
    noise = unit_noise(jax.random.fold_in(key, 23), (REGIONS, OBS_REG, R)) * 6.0
    return jnp.clip(signal + noise, -48.0, 48.0).astype(jnp.bfloat16)


def spd_matrix(key, count, order, level):
    first, second = jax.random.split(jax.random.fold_in(key, 7))
    diag_vals = jax.random.uniform(first, (count, order), jnp.float32, jnp.log(level / 4.0), jnp.log(2.0 * level))
    off_diag = jax.random.normal(second, (count, order, order), jnp.float32) * (level / (16.0 * jnp.sqrt(jnp.float32(order))))
    sym = (off_diag + jnp.swapaxes(off_diag, 1, 2)) * 0.7071
    return sym + jnp.exp(diag_vals)[:, :, None] * jnp.eye(order, dtype=jnp.float32)[None]


def draw_region_prior(key, part):
    return spd_matrix(key, REGIONS, K, 1.0 * OBS_REG).astype(jnp.bfloat16)


def draw_root_prior(key, part):
    return spd_matrix(key, 1, K0, 1.0 * OBS_REG * REGIONS)[0].astype(jnp.bfloat16)


def setup_inputs(seed: int = 0) -> dict:
    key_list = jax.random.split(jax.random.key(seed), 8)
    return {
        "leaf_factor": draw_leaf_factor(jax.random.fold_in(key_list[7], 71), 0),
        "basis_pool": draw_basis_pool(jax.random.fold_in(key_list[7], 71), 0),
        "root_basis": draw_root_basis(jax.random.fold_in(key_list[7], 71), 0),
        "responses": draw_responses(jax.random.fold_in(key_list[7], 71), 0),
        "knot_order": jax.vmap(lambda own: jax.random.permutation(own, POOL))(jax.random.split(key_list[4], REGIONS)).reshape((REGIONS, POOL)).astype(jnp.int32),
        "region_prior": draw_region_prior(jax.random.fold_in(key_list[7], 71), 0),
        "root_prior": draw_root_prior(jax.random.fold_in(key_list[7], 71), 0),
    }


def whiten(leaf_factor_r, pool_cols, root_cols, values, knot_order_r):
    knot_ids = knot_order_r[:K].astype(jnp.int32)
    region_basis = jnp.take(pool_cols, knot_ids, axis=1)
    joined = jnp.concatenate([region_basis, root_cols, values], axis=1)
    blocks = joined.reshape(N_LEAF, LEAF, K + K0 + R).astype(jnp.float32)
    leaf_blocks = leaf_factor_r.reshape(N_LEAF, LEAF, LEAF).astype(jnp.float32)
    white = jnp.einsum('lij,lic->ljc', leaf_blocks, blocks, precision=lax.Precision.HIGHEST)
    return (region_basis, white.astype(jnp.bfloat16))

def region_terms(region_args):
    leaf_factor_r, pool_cols, root_cols, values, knot_order_r, prior_mat = region_args
    region_basis, white = whiten(leaf_factor_r, pool_cols, root_cols, values, knot_order_r)
    white_f = white.astype(jnp.float32)
    gram_b = jnp.einsum('ljk,ljc->kc', white_f[:, :, :K], white_f, precision=lax.Precision.HIGHEST)
    gram_a = jnp.einsum('ljk,ljc->kc', white_f[:, :, K:K + K0], white_f[:, :, K:], precision=lax.Precision.HIGHEST)
    system = prior_mat.astype(jnp.float32) + gram_b[:, :K]
    chol_region = jnp.linalg.cholesky(system)
    solved = jax.scipy.linalg.cho_solve((chol_region, True), gram_b[:, K:])
    correction = gram_a - jnp.dot(gram_b[:, K:K + K0].T, solved, precision=lax.Precision.HIGHEST)
    return (chol_region, solved, correction)

def reference(leaf_factor, basis_pool, root_basis, responses, knot_order, region_prior, root_prior):
    chol_regions, solveds, corrections = lax.map(region_terms, (leaf_factor, basis_pool, root_basis, responses, knot_order, region_prior))
    summed = lax.optimization_barrier(jnp.sum(corrections, axis=0))
    schur_mat = root_prior.astype(jnp.float32) + summed[:, :K0]
    chol_root = jnp.linalg.cholesky(schur_mat)
    root_coef = jax.scipy.linalg.cho_solve((chol_root, True), summed[:, K0:])

    def predict(region_args):
        pool_cols, root_cols, knot_order_r, solved = region_args
        region_basis = jnp.take(pool_cols, knot_order_r[:K].astype(jnp.int32), axis=1)
        region_coef = solved[:, K0:] - jnp.dot(solved[:, :K0], root_coef, precision=lax.Precision.HIGHEST)
        mean_out = jnp.dot(region_basis.astype(jnp.float32), region_coef.astype(jnp.bfloat16).astype(jnp.float32), preferred_element_type=jnp.float32)
        mean_out = mean_out + jnp.dot(root_cols.astype(jnp.float32), root_coef.astype(jnp.bfloat16).astype(jnp.float32), preferred_element_type=jnp.float32)
        return mean_out.astype(jnp.bfloat16)
    predictions = lax.map(predict, (basis_pool, root_basis, knot_order, solveds))
    obs_region = LEAF * N_LEAF
    region_factor = chol_regions / math.sqrt(obs_region)
    root_factor = chol_root / math.sqrt(obs_region * N_REGION)
    return (predictions, region_factor, root_factor)
```

```python
import math

import jax
import jax.numpy as jnp
from jax import lax
from jax.experimental import pallas as pl
from jax.experimental.pallas import tpu as pltpu
from jax.sharding import PartitionSpec as P

STEP = 16
HI = lax.Precision.HIGHEST
F32 = jnp.float32
BF16 = jnp.bfloat16


def rows_dot(left, right, precision=None):
    return lax.dot_general(
        left, right, (((0,), (0,)), ((), ())), precision=precision, preferred_element_type=F32
    )


def one_hot(knots, pool):
    count = knots.shape[1]
    ids = lax.broadcasted_iota(jnp.int32, (pool, count), 0)
    return (ids == knots).astype(BF16)


def grams_kernel(core_ref, knot_ref, factor_ref, pool_ref, root_ref, resp_ref,
                 keep_ref, send_ref, joined, total):
    step = pl.program_id(0)
    knots = total.shape[2] * total.shape[0] * total.shape[1]
    roots = root_ref.shape[2]

    @pl.when(step == 0)
    def _():
        pick = one_hot(knot_ref[:, :knots], pool_ref.shape[2])
        basis = jnp.dot(pool_ref[0], pick, preferred_element_type=F32)
        joined[:, :knots] = basis.astype(BF16)
        joined[:, knots : knots + roots] = root_ref[0]
        joined[:, knots + roots :] = resp_ref[0]
        total[...] = jnp.zeros_like(total)

    white = rows_dot(factor_ref[0], joined[...]).astype(BF16)
    gram_b = rows_dot(white[:, :knots], white)
    gram_a = rows_dot(white[:, knots : knots + roots], white[:, knots:])
    width = gram_b.shape[1]
    total[:, :, :, :width] += gram_b.reshape(*total.shape[:3], width)
    total[:, :, :, width:] += gram_a.reshape(*total.shape[:3], gram_a.shape[1])

    @pl.when(step == pl.num_programs(0) - 1)
    def _():
        core = core_ref[0]
        keep_ref[...] = total[:, core]
        send_ref[...] = total[:, 1 - core]


def split3(x):
    high = x.astype(BF16)
    rest = x - high.astype(F32)
    mid = rest.astype(BF16)
    low = (rest - mid.astype(F32)).astype(BF16)
    return high, mid, low


def factor_inverse(work, diag, panel):
    size = work.shape[0]

    def block(k, _):
        start = pl.multiple_of(k * STEP, STEP)
        tile = pl.multiple_of((start // 128) * 128, 128)
        corner = work[pl.ds(start, STEP), pl.ds(tile, 128)]
        diag[...] = pltpu.roll(corner, lax.rem(128 - (start - tile), 128), 1)
        lane = lax.broadcasted_iota(jnp.int32, (8, size), 1)
        inside = (lane >= start) & (lane < start + STEP)
        d, v = [], []
        for i in range(STEP):
            row = jnp.broadcast_to(diag[i : i + 1, :], (8, 128))
            d.append([None] * i + [jnp.broadcast_to(row[:, j : j + 1], (8, 128)) for j in range(i, STEP)])
            full = jnp.broadcast_to(work[pl.ds(start + i, 1), :], (8, size))
            v.append(jnp.where(inside, jnp.where(lane == start + i, 1.0, 0.0), full))
        for p in range(STEP):
            scale = lax.rsqrt(d[p][p])
            u = [None] * (p + 1) + [d[p][j] * scale for j in range(p + 1, STEP)]
            wide = jnp.concatenate([scale] * (size // 128), axis=1)
            done = v[p] * wide
            panel[p : p + 1, :] = done[0:1, :]
            for i in range(p + 1, STEP):
                for j in range(i, STEP):
                    d[i][j] = d[i][j] - u[i] * u[j]
                v[i] = v[i] - jnp.concatenate([u[i]] * (size // 128), axis=1) * done
        rows = panel[...]
        lane_p = lax.broadcasted_iota(jnp.int32, (STEP, size), 1)
        high, mid, low = split3(rows)
        later = lane_p >= start + STEP
        zero = jnp.zeros_like(high)
        th, tm, tl = (jnp.where(later, x, zero) for x in (high, mid, low))
        left = jnp.concatenate([th, th, tm, th, tl, tm], axis=0)
        right = jnp.concatenate([high, mid, high, low, high, mid], axis=0)
        change = rows_dot(left, right)
        lane_a = lax.broadcasted_iota(jnp.int32, (size, size), 1)
        row_a = lax.broadcasted_iota(jnp.int32, (size, size), 0)
        fresh = (lane_a >= start) & (lane_a < start + STEP) & (row_a >= start + STEP)
        work[...] = jnp.where(fresh, 0.0, work[...]) - change
        work[pl.ds(start, STEP), :] = rows
        return 0

    lax.fori_loop(0, size // STEP, block, 0)
    lane = lax.broadcasted_iota(jnp.int32, (size, size), 1)
    row = lax.broadcasted_iota(jnp.int32, (size, size), 0)
    return jnp.where(lane <= row, work[...], 0.0)


def factor_rows(matrix, first, inverse, scale):
    count = 8
    part = matrix[pl.ds(pl.multiple_of(first, 8), count), :]
    rows = lax.dot_general(
        part, inverse, (((1,), (1,)), ((), ())), precision=HI, preferred_element_type=F32
    )
    lane = lax.broadcasted_iota(jnp.int32, rows.shape, 1)
    row = lax.broadcasted_iota(jnp.int32, rows.shape, 0) + first
    return jnp.where(lane <= row, rows, 0.0) * scale


def region_kernel(scale, leaf_ref, gathered_ref, prior_ref, own_ref,
                  solved_ref, schur_ref, factor_ref, matrix, work, diag, panel, full):
    size = matrix.shape[0]
    first = leaf_ref[0] * 8
    matrix[...] = prior_ref[0].astype(F32) + gathered_ref[:, :size]
    work[...] = matrix[...]
    inverse = factor_inverse(work, diag, panel)
    half = jnp.dot(inverse, gathered_ref[:, size:], precision=HI, preferred_element_type=F32)
    roots = full.shape[0]
    full[...] = rows_dot(half[:, :roots], half, HI)
    schur_ref[...] = own_ref[...] - full[pl.ds(pl.multiple_of(first, 8), 8), :]
    solved_ref[...] = rows_dot(inverse, half, HI)
    factor_ref[0] = factor_rows(matrix, first, inverse, scale)


def root_kernel(scale, leaf_ref, summed_ref, prior_ref, solved_ref, knot_ref, pool_hbm, root_hbm,
                pred_ref, factor_ref, matrix, work, diag, panel, pool, root, sems):
    size = matrix.shape[0]
    loads = [
        pltpu.make_async_copy(pool_hbm.at[0], pool, sems.at[0]),
        pltpu.make_async_copy(root_hbm.at[0], root, sems.at[1]),
    ]
    for load in loads:
        load.start()
    first = leaf_ref[0] * 8
    matrix[...] = prior_ref[...].astype(F32) + summed_ref[:, :size]
    work[...] = matrix[...]
    inverse = factor_inverse(work, diag, panel)
    half = jnp.dot(inverse, summed_ref[:, size:], precision=HI, preferred_element_type=F32)
    root_coef = rows_dot(inverse, half, HI)
    coef = solved_ref[:, size:] - jnp.dot(
        solved_ref[:, :size], root_coef, precision=HI, preferred_element_type=F32
    )
    knots = coef.shape[0]
    pick = one_hot(knot_ref[:, :knots], pool.shape[1])
    spread = jnp.dot(pick, coef.astype(BF16), preferred_element_type=F32).astype(BF16)
    factor_ref[...] = factor_rows(matrix, first, inverse, scale)
    for load in loads:
        load.wait()
    mean = jnp.dot(pool[...], spread, preferred_element_type=F32)
    mean = mean + jnp.dot(root[...], root_coef.astype(BF16), preferred_element_type=F32)
    pred_ref[0] = mean.astype(BF16)


VMEM = pl.BlockSpec(memory_space=pltpu.VMEM)
SMEM = pl.BlockSpec(memory_space=pltpu.SMEM)
ANY = pl.BlockSpec(memory_space=pl.ANY)


def per_device(
    leaf_factor, basis_pool, root_basis, responses, knot_order, region_prior, root_prior
):
    knots = region_prior.shape[1]
    roots = root_prior.shape[0]
    cols = responses.shape[2]
    leaf_count = lax.axis_size("leaf")
    region_count = lax.axis_size("region")
    chips = leaf_count // 2
    rows = leaf_factor.shape[2]
    pool = basis_pool.shape[2]
    leaf = lax.axis_index("leaf").astype(jnp.int32)
    leaf_at = leaf.reshape(1)
    core_at = lax.rem(leaf, 2).reshape(1)
    share = knots // leaf_count
    wide_b = knots + roots + cols
    wide_a = roots + cols
    block = rows // 4

    def fixed(shape):
        return pl.BlockSpec(shape, lambda i: (0,) * len(shape))

    piece = jax.ShapeDtypeStruct((chips, share, wide_b + wide_a), F32)
    keep, send = pl.pallas_call(
        grams_kernel,
        out_shape=(piece, piece),
        grid=(rows // block,),
        in_specs=[
            SMEM,
            fixed(knot_order.shape),
            pl.BlockSpec((1, rows, block), lambda i: (0, 0, i)),
            fixed(basis_pool.shape),
            fixed(root_basis.shape),
            fixed(responses.shape),
        ],
        out_specs=(fixed(piece.shape), fixed(piece.shape)),
        scratch_shapes=[
            pltpu.VMEM((rows, wide_b), BF16),
            pltpu.VMEM((chips, 2, share, wide_b + wide_a), F32),
        ],
        name="grams",
    )(core_at, knot_order, leaf_factor, basis_pool, root_basis, responses)

    swap = [(i, i ^ 1) for i in range(leaf_count)]
    same_core = [list(range(c, leaf_count, 2)) for c in range(2)]
    paired = keep + lax.ppermute(send, "leaf", swap)
    arrived = lax.all_to_all(paired, "leaf", 0, 0, axis_index_groups=same_core, tiled=True)
    own = arrived.sum(axis=0)
    gathered = lax.all_gather(own[:, :wide_b], "leaf", axis=0, tiled=True)

    square = pltpu.VMEM((knots, knots), F32)
    small = [pltpu.VMEM((STEP, 128), F32), pltpu.VMEM((STEP, knots), F32)]
    obs = rows * leaf_count
    solved, schur, region_factor = pl.pallas_call(
        lambda *refs: region_kernel(1.0 / math.sqrt(obs), *refs),
        out_shape=(
            jax.ShapeDtypeStruct((knots, wide_a), F32),
            jax.ShapeDtypeStruct((share, wide_a), F32),
            jax.ShapeDtypeStruct((1, share, knots), F32),
        ),
        in_specs=[SMEM, VMEM, VMEM, VMEM],
        out_specs=(VMEM, VMEM, VMEM),
        scratch_shapes=[square, square, *small, pltpu.VMEM((roots, wide_a), F32)],
        name="region_solve",
    )(leaf_at, gathered, region_prior, own[:, wide_b:])

    copies = jnp.broadcast_to(schur[None], (region_count, *schur.shape))
    summed = lax.all_to_all(copies, "region", 0, 0, tiled=True).sum(axis=0)
    summed = lax.all_gather(summed, "leaf", axis=0, tiled=True)

    predictions, root_factor = pl.pallas_call(
        lambda *refs: root_kernel(1.0 / math.sqrt(obs * region_count), *refs),
        out_shape=(
            jax.ShapeDtypeStruct((1, rows, cols), BF16),
            jax.ShapeDtypeStruct((share, roots), F32),
        ),
        in_specs=[SMEM, VMEM, VMEM, VMEM, VMEM, ANY, ANY],
        out_specs=(VMEM, VMEM),
        scratch_shapes=[
            square, square, *small,
            pltpu.VMEM((rows, pool), BF16),
            pltpu.VMEM((rows, roots), BF16),
            pltpu.SemaphoreType.DMA((2,)),
        ],
        name="root_solve",
    )(leaf_at, summed, root_prior, solved, knot_order, basis_pool, root_basis)
    return predictions, region_factor, root_factor


def solution(mesh):
    placed = (
        P("region", "leaf", None),
        P("region", "leaf", None),
        P("region", "leaf", None),
        P("region", "leaf", None),
        P("region", None),
        P("region", None, None),
        P(),
    )
    return jax.shard_map(
        per_device,
        mesh=mesh,
        in_specs=placed,
        out_specs=(P("region", "leaf", None), P("region", "leaf", None), P("leaf", None)),
        check_vma=False,
    )
```

```python
import math

import jax
import jax.numpy as jnp
from jax import lax
from jax.experimental import pallas as pl
from jax.experimental.pallas import tpu as pltpu
from jax.sharding import PartitionSpec as P

STEP = 16
HI = lax.Precision.HIGHEST
F32 = jnp.float32
BF16 = jnp.bfloat16


def rows_dot(left, right, precision=None):
    return lax.dot_general(
        left, right, (((0,), (0,)), ((), ())), precision=precision, preferred_element_type=F32
    )


def one_hot(knots, pool):
    count = knots.shape[1]
    ids = lax.broadcasted_iota(jnp.int32, (pool, count), 0)
    return (ids == knots).astype(BF16)


def grams_kernel(core_ref, knot_ref, factor_ref, pool_ref, root_ref, resp_ref,
                 keep_b_ref, keep_a_ref, send_ref, joined, total):
    step = pl.program_id(0)
    knots = total.shape[2] * total.shape[0] * total.shape[1]
    roots = root_ref.shape[2]

    @pl.when(step == 0)
    def _():
        pick = one_hot(knot_ref[:, :knots], pool_ref.shape[2])
        basis = jnp.dot(pool_ref[0], pick, preferred_element_type=F32)
        joined[:, :knots] = basis.astype(BF16)
        joined[:, knots : knots + roots] = root_ref[0]
        joined[:, knots + roots :] = resp_ref[0]
        total[...] = jnp.zeros_like(total)

    white = rows_dot(factor_ref[0], joined[...]).astype(BF16)
    gram_b = rows_dot(white[:, :knots], white)
    gram_a = rows_dot(white[:, knots : knots + roots], white[:, knots:])
    width = gram_b.shape[1]
    total[:, :, :, :width] += gram_b.reshape(*total.shape[:3], width)
    total[:, :, :, width:] += gram_a.reshape(*total.shape[:3], gram_a.shape[1])

    @pl.when(step == pl.num_programs(0) - 1)
    def _():
        core = core_ref[0]
        keep = total[:, core]
        keep_b_ref[...] = keep[:, :, : keep_b_ref.shape[2]]
        keep_a_ref[...] = keep[:, :, keep_b_ref.shape[2] :]
        send_ref[...] = total[:, 1 - core]


def pack_kernel(keep_ref, swapped_ref, arrived_ref, out_ref):
    width = keep_ref.shape[2]
    chips = out_ref.shape[0]
    summed = arrived_ref[0]
    for r in range(1, arrived_ref.shape[0]):
        summed = summed + arrived_ref[r]
    piece = summed.shape[1] // chips
    out_ref[:, :, :width] = keep_ref[...] + swapped_ref[:, :, :width]
    for z in range(chips):
        out_ref[z, :, width : width + piece] = summed[:, z * piece : (z + 1) * piece]
        rest = out_ref.shape[2] - width - piece
        out_ref[z, :, width + piece :] = jnp.zeros((summed.shape[0], rest), F32)


def spread_kernel(arrived_ref, own_ref, out_ref):
    summed = arrived_ref[0]
    for r in range(1, arrived_ref.shape[0]):
        summed = summed + arrived_ref[r]
    out_ref[...] = jnp.broadcast_to((own_ref[...] - summed)[None], out_ref.shape)


def split3(x):
    high = x.astype(BF16)
    rest = x - high.astype(F32)
    mid = rest.astype(BF16)
    low = (rest - mid.astype(F32)).astype(BF16)
    return high, mid, low


def factor_inverse(work, diag, panel):
    size = work.shape[0]

    def block(k, _):
        start = pl.multiple_of(k * STEP, STEP)
        tile = pl.multiple_of((start // 128) * 128, 128)
        corner = work[pl.ds(start, STEP), pl.ds(tile, 128)]
        diag[...] = pltpu.roll(corner, lax.rem(128 - (start - tile), 128), 1)
        lane = lax.broadcasted_iota(jnp.int32, (8, size), 1)
        inside = (lane >= start) & (lane < start + STEP)
        d, v = [], []
        for i in range(STEP):
            row = jnp.broadcast_to(diag[i : i + 1, :], (8, 128))
            d.append([None] * i + [jnp.broadcast_to(row[:, j : j + 1], (8, 128)) for j in range(i, STEP)])
            full = jnp.broadcast_to(work[pl.ds(start + i, 1), :], (8, size))
            v.append(jnp.where(inside, jnp.where(lane == start + i, 1.0, 0.0), full))
        for p in range(STEP):
            scale = lax.rsqrt(d[p][p])
            u = [None] * (p + 1) + [d[p][j] * scale for j in range(p + 1, STEP)]
            wide = jnp.concatenate([scale] * (size // 128), axis=1)
            done = v[p] * wide
            panel[p : p + 1, :] = done[0:1, :]
            for i in range(p + 1, STEP):
                for j in range(i, STEP):
                    d[i][j] = d[i][j] - u[i] * u[j]
                v[i] = v[i] - jnp.concatenate([u[i]] * (size // 128), axis=1) * done
        rows = panel[...]
        lane_p = lax.broadcasted_iota(jnp.int32, (STEP, size), 1)
        high, mid, low = split3(rows)
        later = lane_p >= start + STEP
        zero = jnp.zeros_like(high)
        th, tm, tl = (jnp.where(later, x, zero) for x in (high, mid, low))
        left = jnp.concatenate([th, th, tm, th, tl, tm], axis=0)
        right = jnp.concatenate([high, mid, high, low, high, mid], axis=0)
        change = rows_dot(left, right)
        lane_a = lax.broadcasted_iota(jnp.int32, (size, size), 1)
        row_a = lax.broadcasted_iota(jnp.int32, (size, size), 0)
        fresh = (lane_a >= start) & (lane_a < start + STEP) & (row_a >= start + STEP)
        work[...] = jnp.where(fresh, 0.0, work[...]) - change
        work[pl.ds(start, STEP), :] = rows
        return 0

    lax.fori_loop(0, size // STEP, block, 0)
    lane = lax.broadcasted_iota(jnp.int32, (size, size), 1)
    row = lax.broadcasted_iota(jnp.int32, (size, size), 0)
    return jnp.where(lane <= row, work[...], 0.0)


def factor_rows(matrix, first, inverse, scale):
    count = 8
    part = matrix[pl.ds(pl.multiple_of(first, 8), count), :]
    rows = lax.dot_general(
        part, inverse, (((1,), (1,)), ((), ())), precision=HI, preferred_element_type=F32
    )
    lane = lax.broadcasted_iota(jnp.int32, rows.shape, 1)
    row = lax.broadcasted_iota(jnp.int32, rows.shape, 0) + first
    return jnp.where(lane <= row, rows, 0.0) * scale


def region_kernel(scale, leaf_ref, gathered_ref, prior_ref,
                  solved_ref, schur_ref, own_ref, factor_ref, matrix, work, diag, panel):
    size = matrix.shape[0]
    first = leaf_ref[0] * 8
    width = size + solved_ref.shape[1]
    matrix[...] = prior_ref[0].astype(F32) + gathered_ref[:, :size]
    work[...] = matrix[...]
    inverse = factor_inverse(work, diag, panel)
    half = jnp.dot(inverse, gathered_ref[:, size:width], precision=HI, preferred_element_type=F32)
    schur = rows_dot(half[:, : schur_ref.shape[0] * schur_ref.shape[1]], half, HI)
    schur_ref[...] = schur.reshape(schur_ref.shape)
    solved_ref[...] = rows_dot(inverse, half, HI)
    factor_ref[0] = factor_rows(matrix, first, inverse, scale)
    chips = gathered_ref.shape[0] // 16
    piece = own_ref.shape[1] // chips
    for z in range(chips):
        for core in range(2):
            row = (2 * z + core) * 8
            own_ref[core * 8 : core * 8 + 8, z * piece : (z + 1) * piece] = (
                gathered_ref[row : row + 8, width : width + piece]
            )


def root_kernel(scale, leaf_ref, summed_ref, prior_ref, solved_ref, knot_ref, pool_hbm, root_hbm,
                pred_ref, factor_ref, matrix, work, diag, panel, pool, root, sems):
    size = matrix.shape[0]
    loads = [
        pltpu.make_async_copy(pool_hbm.at[0], pool, sems.at[0]),
        pltpu.make_async_copy(root_hbm.at[0], root, sems.at[1]),
    ]
    for load in loads:
        load.start()
    first = leaf_ref[0] * 8
    matrix[...] = prior_ref[...].astype(F32) + summed_ref[:, :size]
    work[...] = matrix[...]
    inverse = factor_inverse(work, diag, panel)
    half = jnp.dot(inverse, summed_ref[:, size:], precision=HI, preferred_element_type=F32)
    root_coef = rows_dot(inverse, half, HI)
    coef = solved_ref[:, size:] - jnp.dot(
        solved_ref[:, :size], root_coef, precision=HI, preferred_element_type=F32
    )
    knots = coef.shape[0]
    pick = one_hot(knot_ref[:, :knots], pool.shape[1])
    spread = jnp.dot(pick, coef.astype(BF16), preferred_element_type=F32).astype(BF16)
    factor_ref[...] = factor_rows(matrix, first, inverse, scale)
    for load in loads:
        load.wait()
    mean = jnp.dot(pool[...], spread, preferred_element_type=F32)
    mean = mean + jnp.dot(root[...], root_coef.astype(BF16), preferred_element_type=F32)
    pred_ref[0] = mean.astype(BF16)


VMEM = pl.BlockSpec(memory_space=pltpu.VMEM)
SMEM = pl.BlockSpec(memory_space=pltpu.SMEM)
ANY = pl.BlockSpec(memory_space=pl.ANY)


def per_device(
    leaf_factor, basis_pool, root_basis, responses, knot_order, region_prior, root_prior
):
    knots = region_prior.shape[1]
    roots = root_prior.shape[0]
    cols = responses.shape[2]
    leaf_count = lax.axis_size("leaf")
    region_count = lax.axis_size("region")
    chips = leaf_count // 2
    rows = leaf_factor.shape[2]
    pool = basis_pool.shape[2]
    leaf = lax.axis_index("leaf").astype(jnp.int32)
    leaf_at = leaf.reshape(1)
    core_at = lax.rem(leaf, 2).reshape(1)
    share = knots // leaf_count
    wide_b = knots + roots + cols
    wide_a = roots + cols
    block = rows // 4

    def fixed(shape):
        return pl.BlockSpec(shape, lambda i: (0,) * len(shape))

    def shape(*dims):
        return jax.ShapeDtypeStruct(dims, F32)

    pieces = (
        shape(chips, share, wide_b),
        shape(chips, share, wide_a),
        shape(chips, share, wide_b + wide_a),
    )
    keep_b, keep_a, send = pl.pallas_call(
        grams_kernel,
        out_shape=pieces,
        grid=(rows // block,),
        in_specs=[
            SMEM,
            fixed(knot_order.shape),
            pl.BlockSpec((1, rows, block), lambda i: (0, 0, i)),
            fixed(basis_pool.shape),
            fixed(root_basis.shape),
            fixed(responses.shape),
        ],
        out_specs=tuple(fixed(p.shape) for p in pieces),
        scratch_shapes=[
            pltpu.VMEM((rows, wide_b), BF16),
            pltpu.VMEM((chips, 2, share, wide_b + wide_a), F32),
        ],
        name="grams",
    )(core_at, knot_order, leaf_factor, basis_pool, root_basis, responses)

    swap = [(i, i ^ 1) for i in range(leaf_count)]
    same_core = [list(range(c, leaf_count, 2)) for c in range(2)]
    swapped = lax.ppermute(send, "leaf", swap)
    root_part = lax.all_to_all(keep_a + swapped[:, :, wide_b:], "region", 0, 0, tiled=True)
    packed = pl.pallas_call(
        pack_kernel,
        out_shape=shape(chips, share, wide_b + 128),
        in_specs=[VMEM, VMEM, VMEM],
        out_specs=VMEM,
        name="pack",
    )(keep_b, swapped, root_part)
    arrived = lax.all_to_all(packed, "leaf", 0, 0, axis_index_groups=same_core, tiled=True)
    gathered = lax.all_gather(arrived.sum(axis=0), "leaf", axis=0, tiled=True)

    square = pltpu.VMEM((knots, knots), F32)
    small = [pltpu.VMEM((STEP, 128), F32), pltpu.VMEM((STEP, knots), F32)]
    obs = rows * leaf_count
    chunk = roots // region_count
    solved, schur, own, region_factor = pl.pallas_call(
        lambda *refs: region_kernel(1.0 / math.sqrt(obs), *refs),
        out_shape=(
            shape(knots, wide_a),
            shape(region_count, chunk, wide_a),
            shape(chunk, wide_a),
            shape(1, share, knots),
        ),
        in_specs=[SMEM, VMEM, VMEM],
        out_specs=(VMEM,) * 4,
        scratch_shapes=[square, square, *small],
        name="region_solve",
    )(leaf_at, gathered, region_prior)

    schur = lax.all_to_all(schur, "region", 0, 0, tiled=True)
    copies = pl.pallas_call(
        spread_kernel,
        out_shape=shape(region_count, chunk, wide_a),
        in_specs=[VMEM, VMEM],
        out_specs=VMEM,
        name="spread",
    )(schur, own)
    summed = lax.all_to_all(copies, "region", 0, 0, tiled=True).reshape(roots, wide_a)

    predictions, root_factor = pl.pallas_call(
        lambda *refs: root_kernel(1.0 / math.sqrt(obs * region_count), *refs),
        out_shape=(
            jax.ShapeDtypeStruct((1, rows, cols), BF16),
            jax.ShapeDtypeStruct((share, roots), F32),
        ),
        in_specs=[SMEM, VMEM, VMEM, VMEM, VMEM, ANY, ANY],
        out_specs=(VMEM, VMEM),
        scratch_shapes=[
            square, square, *small,
            pltpu.VMEM((rows, pool), BF16),
            pltpu.VMEM((rows, roots), BF16),
            pltpu.SemaphoreType.DMA((2,)),
        ],
        name="root_solve",
    )(leaf_at, summed, root_prior, solved, knot_order, basis_pool, root_basis)
    return predictions, region_factor, root_factor


def solution(mesh):
    placed = (
        P("region", "leaf", None),
        P("region", "leaf", None),
        P("region", "leaf", None),
        P("region", "leaf", None),
        P("region", None),
        P("region", None, None),
        P(),
    )
    return jax.shard_map(
        per_device,
        mesh=mesh,
        in_specs=placed,
        out_specs=(P("region", "leaf", None), P("region", "leaf", None), P("leaf", None)),
        check_vma=False,
    )
```

```python
import math

import jax
import jax.numpy as jnp
from jax import lax
from jax.experimental import pallas as pl
from jax.experimental.pallas import tpu as pltpu
from jax.sharding import PartitionSpec as P

STEP = 16
HI = lax.Precision.HIGHEST
F32 = jnp.float32
BF16 = jnp.bfloat16


def rows_dot(left, right, precision=None):
    return lax.dot_general(
        left, right, (((0,), (0,)), ((), ())), precision=precision, preferred_element_type=F32
    )


def one_hot(knots, pool):
    count = knots.shape[1]
    ids = lax.broadcasted_iota(jnp.int32, (pool, count), 0)
    return (ids == knots).astype(BF16)


def grams_kernel(core_ref, knot_ref, factor_ref, pool_ref, root_ref, resp_ref,
                 keep_b_ref, keep_a_ref, send_ref, joined, total_b, total_a):
    step = pl.program_id(0)
    width = total_b.shape[3]
    roots = root_ref.shape[2]
    knots = width - total_a.shape[3]

    @pl.when(step == 0)
    def _():
        pick = one_hot(knot_ref[:, :knots], pool_ref.shape[2])
        basis = jnp.dot(pool_ref[0], pick, preferred_element_type=F32)
        joined[:, :knots] = basis.astype(BF16)
        joined[:, knots : knots + roots] = root_ref[0]
        joined[:, knots + roots :] = resp_ref[0]
        total_b[...] = jnp.zeros_like(total_b)
        total_a[...] = jnp.zeros_like(total_a)

    white = rows_dot(factor_ref[0], joined[...]).astype(BF16)
    total_b[...] += rows_dot(white[:, :knots], white).reshape(total_b.shape)
    total_a[...] += rows_dot(white[:, knots : knots + roots], white[:, knots:]).reshape(
        total_a.shape
    )

    @pl.when(step == pl.num_programs(0) - 1)
    def _():
        core = core_ref[0]
        keep_b_ref[...] = total_b[core]
        keep_a_ref[...] = total_a[:, core]
        send_ref[:, :, :width] = total_b[1 - core]
        send_ref[:, :, width:] = total_a[:, 1 - core]


def pack_kernel(keep_ref, swapped_ref, arrived_ref, out_ref):
    width = keep_ref.shape[2]
    chips = out_ref.shape[0]
    summed = arrived_ref[0]
    for r in range(1, arrived_ref.shape[0]):
        summed = summed + arrived_ref[r]
    piece = summed.shape[1] // chips
    out_ref[:, :, :width] = keep_ref[...] + swapped_ref[:, :, :width]
    for z in range(chips):
        out_ref[z, :, width : width + piece] = summed[:, z * piece : (z + 1) * piece]
        rest = out_ref.shape[2] - width - piece
        out_ref[z, :, width + piece :] = jnp.zeros((summed.shape[0], rest), F32)


def spread_kernel(arrived_ref, own_ref, out_ref):
    summed = arrived_ref[0]
    for r in range(1, arrived_ref.shape[0]):
        summed = summed + arrived_ref[r]
    out_ref[...] = jnp.broadcast_to((own_ref[...] - summed)[None], out_ref.shape)


def split3(x):
    high = x.astype(BF16)
    rest = x - high.astype(F32)
    mid = rest.astype(BF16)
    low = (rest - mid.astype(F32)).astype(BF16)
    return high, mid, low


def split_dot(left, right, dims, terms=6):
    lh, lm, ll = split3(left)
    rh, rm, rl = split3(right)
    lefts = jnp.concatenate([lh, lh, lm, lh, ll, lm][:terms], axis=dims[0])
    rights = jnp.concatenate([rh, rm, rh, rl, rh, rm][:terms], axis=dims[1])
    return lax.dot_general(
        lefts, rights, (((dims[0],), (dims[1],)), ((), ())), preferred_element_type=F32
    )


def factor_inverse(work, diag, panel):
    size = work.shape[0]
    tiles = size // 128

    def block(k, _):
        start = pl.multiple_of(k * STEP, STEP)
        tile = pl.multiple_of((start // 128) * 128, 128)
        corner = work[pl.ds(start, STEP), pl.ds(tile, 128)]
        diag[...] = pltpu.roll(corner, lax.rem(128 - (start - tile), 128), 1)
        held = work[pl.ds(start, STEP), :]
        sub = lax.broadcasted_iota(jnp.int32, (8, 128), 0)
        at = sub * 128 + lax.broadcasted_iota(jnp.int32, (8, 128), 1) - start
        inside = (at >= 0) & (at < STEP)
        d, v = [], []
        for i in range(STEP):
            row = jnp.broadcast_to(diag[i : i + 1, :], (8, 128))
            d.append([None] * i + [jnp.broadcast_to(row[:, j : j + 1], (8, 128)) for j in range(i, STEP)])
            full = jnp.broadcast_to(held[i : i + 1, 0:128], (8, 128))
            for t in range(1, tiles):
                more = held[i : i + 1, t * 128 : (t + 1) * 128]
                full = jnp.where(sub == t, jnp.broadcast_to(more, (8, 128)), full)
            v.append(jnp.where(inside, jnp.where(at == i, 1.0, 0.0), full))
        for p in range(STEP):
            scale = lax.rsqrt(d[p][p])
            u = [None] * (p + 1) + [d[p][j] * scale for j in range(p + 1, STEP)]
            done = v[p] * scale
            panel[tiles * p : tiles * (p + 1), :] = done[0:tiles, :]
            for i in range(p + 1, STEP):
                for j in range(i, STEP):
                    d[i][j] = d[i][j] - u[i] * u[j]
                v[i] = v[i] - u[i] * done
        rows = jnp.concatenate(
            [panel[pl.ds(t, STEP, stride=tiles), :] for t in range(tiles)], axis=1
        )
        lane_p = lax.broadcasted_iota(jnp.int32, (STEP, size), 1)
        high, mid, low = split3(rows)
        later = lane_p >= start + STEP
        zero = jnp.zeros_like(high)
        th, tm, tl = (jnp.where(later, x, zero) for x in (high, mid, low))
        left = jnp.concatenate([th, th, tm, th, tl, tm], axis=0)
        right = jnp.concatenate([high, mid, high, low, high, mid], axis=0)
        change = rows_dot(left, right)
        lane_a = lax.broadcasted_iota(jnp.int32, (size, size), 1)
        row_a = lax.broadcasted_iota(jnp.int32, (size, size), 0)
        fresh = (lane_a >= start) & (lane_a < start + STEP) & (row_a >= start + STEP)
        work[...] = jnp.where(fresh, 0.0, work[...]) - change
        work[pl.ds(start, STEP), :] = rows
        return 0

    lax.fori_loop(0, size // STEP, block, 0)
    lane = lax.broadcasted_iota(jnp.int32, (size, size), 1)
    row = lax.broadcasted_iota(jnp.int32, (size, size), 0)
    return jnp.where(lane <= row, work[...], 0.0)


def factor_rows(matrix, first, inverse, scale):
    count = 8
    part = matrix[pl.ds(pl.multiple_of(first, 8), count), :]
    rows = split_dot(part, inverse, (1, 1), 3)
    lane = lax.broadcasted_iota(jnp.int32, rows.shape, 1)
    row = lax.broadcasted_iota(jnp.int32, rows.shape, 0) + first
    return jnp.where(lane <= row, rows, 0.0) * scale


def region_kernel(scale, leaf_ref, gathered_ref, prior_ref,
                  solved_ref, schur_ref, own_ref, factor_ref, matrix, work, diag, panel):
    size = matrix.shape[0]
    first = leaf_ref[0] * 8
    width = size + solved_ref.shape[1]
    matrix[...] = prior_ref[0].astype(F32) + gathered_ref[:, :size]
    work[...] = matrix[...]
    inverse = factor_inverse(work, diag, panel)
    half = split_dot(inverse, gathered_ref[:, size:width], (1, 0))
    schur = split_dot(half[:, : schur_ref.shape[0] * schur_ref.shape[1]], half, (0, 0))
    schur_ref[...] = schur.reshape(schur_ref.shape)
    solved_ref[...] = split_dot(inverse, half, (0, 0), 3)
    factor_ref[0] = factor_rows(matrix, first, inverse, scale)
    chips = gathered_ref.shape[0] // 16
    piece = own_ref.shape[1] // chips
    for z in range(chips):
        for core in range(2):
            row = (core * chips + z) * 8
            own_ref[core * 8 : core * 8 + 8, z * piece : (z + 1) * piece] = (
                gathered_ref[row : row + 8, width : width + piece]
            )


def root_kernel(scale, leaf_ref, summed_ref, prior_ref, solved_ref, knot_ref, pool_hbm, root_hbm,
                pred_ref, factor_ref, matrix, work, diag, panel, pool, root, sems):
    size = matrix.shape[0]
    loads = [
        pltpu.make_async_copy(pool_hbm.at[0], pool, sems.at[0]),
        pltpu.make_async_copy(root_hbm.at[0], root, sems.at[1]),
    ]
    for load in loads:
        load.start()
    first = leaf_ref[0] * 8
    matrix[...] = prior_ref[...].astype(F32) + summed_ref[:, :size]
    work[...] = matrix[...]
    inverse = factor_inverse(work, diag, panel)
    half = split_dot(inverse, summed_ref[:, size:], (1, 0), 3)
    root_coef = split_dot(inverse, half, (0, 0), 3)
    coef = solved_ref[:, size:] - split_dot(solved_ref[:, :size], root_coef, (1, 0), 3)
    knots = coef.shape[0]
    pick = one_hot(knot_ref[:, :knots], pool.shape[1])
    spread = jnp.dot(pick, coef.astype(BF16), preferred_element_type=F32).astype(BF16)
    factor_ref[...] = factor_rows(matrix, first, inverse, scale)
    for load in loads:
        load.wait()
    mean = jnp.dot(pool[...], spread, preferred_element_type=F32)
    mean = mean + jnp.dot(root[...], root_coef.astype(BF16), preferred_element_type=F32)
    pred_ref[0] = mean.astype(BF16)


VMEM = pl.BlockSpec(memory_space=pltpu.VMEM)
SMEM = pl.BlockSpec(memory_space=pltpu.SMEM)
ANY = pl.BlockSpec(memory_space=pl.ANY)


def per_device(
    leaf_factor, basis_pool, root_basis, responses, knot_order, region_prior, root_prior
):
    knots = region_prior.shape[1]
    roots = root_prior.shape[0]
    cols = responses.shape[2]
    leaf_count = lax.axis_size("leaf")
    region_count = lax.axis_size("region")
    chips = leaf_count // 2
    rows = leaf_factor.shape[2]
    pool = basis_pool.shape[2]
    leaf = lax.axis_index("leaf").astype(jnp.int32)
    leaf_at = leaf.reshape(1)
    core_at = lax.rem(leaf, 2).reshape(1)
    share = knots // leaf_count
    wide_b = knots + roots + cols
    wide_a = roots + cols
    block = rows // 4

    def fixed(shape):
        return pl.BlockSpec(shape, lambda i: (0,) * len(shape))

    def shape(*dims):
        return jax.ShapeDtypeStruct(dims, F32)

    pieces = (
        shape(chips, share, wide_b),
        shape(chips, share, wide_a),
        shape(chips, share, wide_b + wide_a),
    )
    keep_b, keep_a, send = pl.pallas_call(
        grams_kernel,
        out_shape=pieces,
        grid=(rows // block,),
        in_specs=[
            SMEM,
            fixed(knot_order.shape),
            pl.BlockSpec((1, rows, block), lambda i: (0, 0, i)),
            fixed(basis_pool.shape),
            fixed(root_basis.shape),
            fixed(responses.shape),
        ],
        out_specs=tuple(fixed(p.shape) for p in pieces),
        scratch_shapes=[
            pltpu.VMEM((rows, wide_b), BF16),
            pltpu.VMEM((2, chips, share, wide_b), F32),
            pltpu.VMEM((chips, 2, share, wide_a), F32),
        ],
        name="grams",
    )(core_at, knot_order, leaf_factor, basis_pool, root_basis, responses)

    swap = [(i, i ^ 1) for i in range(leaf_count)]
    same_core = [list(range(c, leaf_count, 2)) for c in range(2)]
    swapped = lax.ppermute(send, "leaf", swap)
    root_part = lax.all_to_all(keep_a + swapped[:, :, wide_b:], "region", 0, 0, tiled=True)
    packed = pl.pallas_call(
        pack_kernel,
        out_shape=shape(chips, share, wide_b + 128),
        in_specs=[VMEM, VMEM, VMEM],
        out_specs=VMEM,
        name="pack",
    )(keep_b, swapped, root_part)
    arrived = lax.all_to_all(packed, "leaf", 0, 0, axis_index_groups=same_core, tiled=True)
    copies = jnp.broadcast_to(arrived.sum(axis=0)[None], arrived.shape)
    column = lax.all_to_all(copies, "leaf", 0, 0, axis_index_groups=same_core, tiled=True)
    column = column.reshape(chips * share, column.shape[2])
    same_chip = [[i, i + 1] for i in range(0, leaf_count, 2)]
    gathered = lax.all_gather(column, "leaf", axis=0, axis_index_groups=same_chip, tiled=True)

    square = pltpu.VMEM((knots, knots), F32)
    small = [pltpu.VMEM((STEP, 128), F32), pltpu.VMEM((STEP * knots // 128, 128), F32)]
    obs = rows * leaf_count
    chunk = roots // region_count
    solved, schur, own, region_factor = pl.pallas_call(
        lambda *refs: region_kernel(1.0 / math.sqrt(obs), *refs),
        out_shape=(
            shape(knots, wide_a),
            shape(region_count, chunk, wide_a),
            shape(chunk, wide_a),
            shape(1, share, knots),
        ),
        in_specs=[SMEM, VMEM, VMEM],
        out_specs=(VMEM,) * 4,
        scratch_shapes=[square, square, *small],
        name="region_solve",
    )(leaf_at, gathered, region_prior)

    schur = lax.all_to_all(schur, "region", 0, 0, tiled=True)
    copies = pl.pallas_call(
        spread_kernel,
        out_shape=shape(region_count, chunk, wide_a),
        in_specs=[VMEM, VMEM],
        out_specs=VMEM,
        name="spread",
    )(schur, own)
    summed = lax.all_to_all(copies, "region", 0, 0, tiled=True).reshape(roots, wide_a)

    predictions, root_factor = pl.pallas_call(
        lambda *refs: root_kernel(1.0 / math.sqrt(obs * region_count), *refs),
        out_shape=(
            jax.ShapeDtypeStruct((1, rows, cols), BF16),
            jax.ShapeDtypeStruct((share, roots), F32),
        ),
        in_specs=[SMEM, VMEM, VMEM, VMEM, VMEM, ANY, ANY],
        out_specs=(VMEM, VMEM),
        scratch_shapes=[
            square, square, *small,
            pltpu.VMEM((rows, pool), BF16),
            pltpu.VMEM((rows, roots), BF16),
            pltpu.SemaphoreType.DMA((2,)),
        ],
        name="root_solve",
    )(leaf_at, summed, root_prior, solved, knot_order, basis_pool, root_basis)
    return predictions, region_factor, root_factor


def solution(mesh):
    placed = (
        P("region", "leaf", None),
        P("region", "leaf", None),
        P("region", "leaf", None),
        P("region", "leaf", None),
        P("region", None),
        P("region", None, None),
        P(),
    )
    return jax.shard_map(
        per_device,
        mesh=mesh,
        in_specs=placed,
        out_specs=(P("region", "leaf", None), P("region", "leaf", None), P("leaf", None)),
        check_vma=False,
    )
```

```python
import math

import jax
import jax.numpy as jnp
from jax import lax
from jax.experimental import pallas as pl
from jax.experimental.pallas import tpu as pltpu
from jax.sharding import PartitionSpec as P

STEP = 16
HI = lax.Precision.HIGHEST
F32 = jnp.float32
BF16 = jnp.bfloat16


def rows_dot(left, right, precision=None):
    return lax.dot_general(
        left, right, (((0,), (0,)), ((), ())), precision=precision, preferred_element_type=F32
    )


def one_hot(knots, pool):
    count = knots.shape[1]
    ids = lax.broadcasted_iota(jnp.int32, (pool, count), 0)
    return (ids == knots).astype(BF16)


def grams_kernel(core_ref, knot_ref, factor_hbm, pool_hbm, root_hbm, resp_hbm,
                 keep_ref, send_ref, joined, factor, pool, total, sems):
    roots = root_hbm.shape[2]
    width = joined.shape[1]
    knots = width - roots - resp_hbm.shape[2]
    loads = [
        pltpu.make_async_copy(pool_hbm.at[0], pool, sems.at[0]),
        pltpu.make_async_copy(root_hbm.at[0], joined.at[:, pl.ds(knots, roots)], sems.at[1]),
        pltpu.make_async_copy(
            resp_hbm.at[0], joined.at[:, pl.ds(knots + roots, width - knots - roots)], sems.at[2]
        ),
        pltpu.make_async_copy(factor_hbm.at[0], factor, sems.at[3]),
    ]
    for load in loads:
        load.start()
    pick = one_hot(knot_ref[:, :knots], pool.shape[1])
    loads[0].wait()
    basis = jnp.dot(pool[...], pick, preferred_element_type=F32)
    joined[:, :knots] = basis.astype(BF16)
    for load in loads[1:]:
        load.wait()
    white = rows_dot(factor[...], joined[...]).astype(BF16)
    gram_b = rows_dot(white[:, :knots], white)
    gram_a = rows_dot(white[:, knots : knots + roots], white[:, knots:])
    total[:, :, :, :width] = gram_b.reshape(*total.shape[:3], width)
    total[:, :, :, width:] = gram_a.reshape(*total.shape[:3], gram_a.shape[1])
    core = core_ref[0]
    keep_ref[...] = total[core]
    send_ref[...] = total[1 - core]


def split3(x):
    high = x.astype(BF16)
    rest = x - high.astype(F32)
    mid = rest.astype(BF16)
    low = (rest - mid.astype(F32)).astype(BF16)
    return high, mid, low


def split_dot(left, right, dims, terms=6):
    lh, lm, ll = split3(left)
    rh, rm, rl = split3(right)
    lefts = jnp.concatenate([lh, lh, lm, lh, ll, lm][:terms], axis=dims[0])
    rights = jnp.concatenate([rh, rm, rh, rl, rh, rm][:terms], axis=dims[1])
    return lax.dot_general(
        lefts, rights, (((dims[0],), (dims[1],)), ((), ())), preferred_element_type=F32
    )


def factor_inverse(work, diag, panel):
    size = work.shape[0]
    tiles = size // 128

    def block(k, _):
        start = pl.multiple_of(k * STEP, STEP)
        tile = pl.multiple_of((start // 128) * 128, 128)
        corner = work[pl.ds(start, STEP), pl.ds(tile, 128)]
        diag[...] = pltpu.roll(corner, lax.rem(128 - (start - tile), 128), 1)
        held = work[pl.ds(start, STEP), :]
        sub = lax.broadcasted_iota(jnp.int32, (8, 128), 0)
        at = sub * 128 + lax.broadcasted_iota(jnp.int32, (8, 128), 1) - start
        inside = (at >= 0) & (at < STEP)
        d, v = [], []
        for i in range(STEP):
            row = jnp.broadcast_to(diag[i : i + 1, :], (8, 128))
            d.append([None] * i + [jnp.broadcast_to(row[:, j : j + 1], (8, 128)) for j in range(i, STEP)])
            full = jnp.broadcast_to(held[i : i + 1, 0:128], (8, 128))
            for t in range(1, tiles):
                more = held[i : i + 1, t * 128 : (t + 1) * 128]
                full = jnp.where(sub == t, jnp.broadcast_to(more, (8, 128)), full)
            v.append(jnp.where(inside, jnp.where(at == i, 1.0, 0.0), full))
        for p in range(STEP):
            scale = lax.rsqrt(d[p][p])
            u = [None] * (p + 1) + [d[p][j] * scale for j in range(p + 1, STEP)]
            done = v[p] * scale
            panel[tiles * p : tiles * (p + 1), :] = done[0:tiles, :]
            for i in range(p + 1, STEP):
                for j in range(i, STEP):
                    d[i][j] = d[i][j] - u[i] * u[j]
                v[i] = v[i] - u[i] * done
        rows = jnp.concatenate(
            [panel[pl.ds(t, STEP, stride=tiles), :] for t in range(tiles)], axis=1
        )
        lane_p = lax.broadcasted_iota(jnp.int32, (STEP, size), 1)
        high, mid, low = split3(rows)
        later = lane_p >= start + STEP
        zero = jnp.zeros_like(high)
        th, tm, tl = (jnp.where(later, x, zero) for x in (high, mid, low))
        left = jnp.concatenate([th, th, tm, th, tl, tm], axis=0)
        right = jnp.concatenate([high, mid, high, low, high, mid], axis=0)
        change = rows_dot(left, right)
        lane_a = lax.broadcasted_iota(jnp.int32, (size, size), 1)
        row_a = lax.broadcasted_iota(jnp.int32, (size, size), 0)
        fresh = (lane_a >= start) & (lane_a < start + STEP) & (row_a >= start + STEP)
        work[...] = jnp.where(fresh, 0.0, work[...]) - change
        work[pl.ds(start, STEP), :] = rows
        return 0

    lax.fori_loop(0, size // STEP, block, 0)
    lane = lax.broadcasted_iota(jnp.int32, (size, size), 1)
    row = lax.broadcasted_iota(jnp.int32, (size, size), 0)
    return jnp.where(lane <= row, work[...], 0.0)


def factor_rows(matrix, first, inverse, scale):
    count = 8
    part = matrix[pl.ds(pl.multiple_of(first, 8), count), :]
    rows = split_dot(part, inverse, (1, 1), 3)
    lane = lax.broadcasted_iota(jnp.int32, rows.shape, 1)
    row = lax.broadcasted_iota(jnp.int32, rows.shape, 0) + first
    return jnp.where(lane <= row, rows, 0.0) * scale


def region_kernel(scale, leaf_ref, gathered_ref, column_ref, prior_ref,
                  solved_ref, schur_ref, factor_ref, matrix, work, diag, panel, half_ref):
    size = matrix.shape[0]
    first = leaf_ref[0] * 8
    width = size + solved_ref.shape[1]
    count = schur_ref.shape[0] * schur_ref.shape[1]
    mine = pl.multiple_of(lax.rem(leaf_ref[0], 2) * count, count)
    matrix[...] = prior_ref[0].astype(F32) + gathered_ref[:, :size]
    work[...] = matrix[...]
    inverse = factor_inverse(work, diag, panel)
    half = split_dot(inverse, gathered_ref[:, size:width], (1, 0))
    half_ref[...] = half
    schur = column_ref[:, width:] - split_dot(
        half_ref[:, pl.ds(mine, count)], half, (0, 0)
    )
    schur_ref[...] = schur.reshape(schur_ref.shape)
    solved_ref[...] = split_dot(inverse, half, (0, 0), 3)
    factor_ref[0] = factor_rows(matrix, first, inverse, scale)


def root_kernel(scale, leaf_ref, summed_ref, prior_ref, solved_ref, knot_ref, pool_hbm, root_hbm,
                pred_ref, factor_ref, matrix, work, diag, panel, pool, root, sems):
    size = matrix.shape[0]
    loads = [
        pltpu.make_async_copy(pool_hbm.at[0], pool, sems.at[0]),
        pltpu.make_async_copy(root_hbm.at[0], root, sems.at[1]),
    ]
    for load in loads:
        load.start()
    first = leaf_ref[0] * 8
    matrix[...] = prior_ref[...].astype(F32) + summed_ref[:, :size]
    work[...] = matrix[...]
    inverse = factor_inverse(work, diag, panel)
    half = split_dot(inverse, summed_ref[:, size:], (1, 0), 3)
    root_coef = split_dot(inverse, half, (0, 0), 3)
    coef = solved_ref[:, size:] - split_dot(solved_ref[:, :size], root_coef, (1, 0), 3)
    knots = coef.shape[0]
    pick = one_hot(knot_ref[:, :knots], pool.shape[1])
    spread = jnp.dot(pick, coef.astype(BF16), preferred_element_type=F32).astype(BF16)
    factor_ref[...] = factor_rows(matrix, first, inverse, scale)
    for load in loads:
        load.wait()
    mean = jnp.dot(pool[...], spread, preferred_element_type=F32)
    mean = mean + jnp.dot(root[...], root_coef.astype(BF16), preferred_element_type=F32)
    pred_ref[0] = mean.astype(BF16)


VMEM = pl.BlockSpec(memory_space=pltpu.VMEM)
SMEM = pl.BlockSpec(memory_space=pltpu.SMEM)
ANY = pl.BlockSpec(memory_space=pl.ANY)


def per_device(
    leaf_factor, basis_pool, root_basis, responses, knot_order, region_prior, root_prior
):
    knots = region_prior.shape[1]
    roots = root_prior.shape[0]
    cols = responses.shape[2]
    leaf_count = lax.axis_size("leaf")
    region_count = lax.axis_size("region")
    chips = leaf_count // 2
    rows = leaf_factor.shape[2]
    pool = basis_pool.shape[2]
    leaf = lax.axis_index("leaf").astype(jnp.int32)
    leaf_at = leaf.reshape(1)
    core_at = lax.rem(leaf, 2).reshape(1)
    share = knots // leaf_count
    wide_b = knots + roots + cols
    wide_a = roots + cols

    def shape(*dims):
        return jax.ShapeDtypeStruct(dims, F32)

    piece = shape(chips, share, wide_b + wide_a)
    keep, send = pl.pallas_call(
        grams_kernel,
        out_shape=(piece, piece),
        in_specs=[SMEM, VMEM, ANY, ANY, ANY, ANY],
        out_specs=(VMEM, VMEM),
        scratch_shapes=[
            pltpu.VMEM((rows, wide_b), BF16),
            pltpu.VMEM((rows, rows), BF16),
            pltpu.VMEM((rows, pool), BF16),
            pltpu.VMEM((2, chips, share, wide_b + wide_a), F32),
            pltpu.SemaphoreType.DMA((4,)),
        ],
        name="grams",
    )(core_at, knot_order, leaf_factor, basis_pool, root_basis, responses)

    swap = [(i, i ^ 1) for i in range(leaf_count)]
    same_core = [list(range(c, leaf_count, 2)) for c in range(2)]
    same_chip = [[i, i + 1] for i in range(0, leaf_count, 2)]
    paired = keep + lax.ppermute(send, "leaf", swap)
    arrived = lax.all_to_all(paired, "leaf", 0, 0, axis_index_groups=same_core, tiled=True)
    column = lax.all_gather(
        arrived.sum(axis=0), "leaf", axis=0, axis_index_groups=same_core, tiled=True
    )
    gathered = lax.all_gather(
        column[:, :wide_b], "leaf", axis=0, axis_index_groups=same_chip, tiled=True
    )

    square = pltpu.VMEM((knots, knots), F32)
    small = [pltpu.VMEM((STEP, 128), F32), pltpu.VMEM((STEP * knots // 128, 128), F32)]
    obs = rows * leaf_count
    chunk = roots // region_count // 2
    part = shape(region_count, chunk, wide_a)
    solved, schur, region_factor = pl.pallas_call(
        lambda *refs: region_kernel(1.0 / math.sqrt(obs), *refs),
        out_shape=(shape(knots, wide_a), part, shape(1, share, knots)),
        in_specs=[SMEM, VMEM, VMEM, VMEM],
        out_specs=(VMEM,) * 3,
        scratch_shapes=[square, square, *small, pltpu.VMEM((knots, wide_a), F32)],
        name="region_solve",
    )(leaf_at, gathered, column, region_prior)

    schur = lax.all_to_all(schur, "region", 0, 0, tiled=True)
    copies = jnp.broadcast_to(schur.sum(axis=0)[None], part.shape)
    summed = lax.all_to_all(copies, "region", 0, 0, tiled=True).reshape(roots // 2, wide_a)
    summed = lax.all_gather(summed, "leaf", axis=0, axis_index_groups=same_chip, tiled=True)

    predictions, root_factor = pl.pallas_call(
        lambda *refs: root_kernel(1.0 / math.sqrt(obs * region_count), *refs),
        out_shape=(
            jax.ShapeDtypeStruct((1, rows, cols), BF16),
            jax.ShapeDtypeStruct((share, roots), F32),
        ),
        in_specs=[SMEM, VMEM, VMEM, VMEM, VMEM, ANY, ANY],
        out_specs=(VMEM, VMEM),
        scratch_shapes=[
            square, square, *small,
            pltpu.VMEM((rows, pool), BF16),
            pltpu.VMEM((rows, roots), BF16),
            pltpu.SemaphoreType.DMA((2,)),
        ],
        name="root_solve",
    )(leaf_at, summed, root_prior, solved, knot_order, basis_pool, root_basis)
    return predictions, region_factor, root_factor


def solution(mesh):
    placed = (
        P("region", "leaf", None),
        P("region", "leaf", None),
        P("region", "leaf", None),
        P("region", "leaf", None),
        P("region", None),
        P("region", None, None),
        P(),
    )
    return jax.shard_map(
        per_device,
        mesh=mesh,
        in_specs=placed,
        out_specs=(P("region", "leaf", None), P("region", "leaf", None), P("leaf", None)),
        check_vma=False,
    )
```

```python
import functools
import math

import jax
import jax.numpy as jnp
from jax import lax
from jax.experimental import pallas as pl
from jax.experimental.pallas import tpu as pltpu
from jax.sharding import PartitionSpec as P

STEP = 16
HI = lax.Precision.HIGHEST
F32 = jnp.float32
BF16 = jnp.bfloat16


def rows_dot(left, right, precision=None):
    return lax.dot_general(
        left, right, (((0,), (0,)), ((), ())), precision=precision, preferred_element_type=F32
    )


def one_hot(knots, pool):
    count = knots.shape[1]
    ids = lax.broadcasted_iota(jnp.int32, (pool, count), 0)
    return (ids == knots).astype(BF16)


def grams_kernel(core_ref, knot_ref, factor_hbm, pool_hbm, root_hbm, resp_hbm,
                 keep_ref, send_ref, joined, factor, pool, total, sems):
    roots = root_hbm.shape[2]
    width = joined.shape[1]
    knots = width - roots - resp_hbm.shape[2]
    loads = [
        pltpu.make_async_copy(pool_hbm.at[0], pool, sems.at[0]),
        pltpu.make_async_copy(root_hbm.at[0], joined.at[:, pl.ds(knots, roots)], sems.at[1]),
        pltpu.make_async_copy(
            resp_hbm.at[0], joined.at[:, pl.ds(knots + roots, width - knots - roots)], sems.at[2]
        ),
        pltpu.make_async_copy(factor_hbm.at[0], factor, sems.at[3]),
    ]
    for load in loads:
        load.start()
    pick = one_hot(knot_ref[:, :knots], pool.shape[1])
    loads[0].wait()
    basis = jnp.dot(pool[...], pick, preferred_element_type=F32)
    joined[:, :knots] = basis.astype(BF16)
    for load in loads[1:]:
        load.wait()
    white = rows_dot(factor[...], joined[...]).astype(BF16)
    gram_b = rows_dot(white[:, :knots], white)
    gram_a = rows_dot(white[:, knots : knots + roots], white[:, knots:])
    rows = knots // 2
    for side in range(2):
        mine = slice(side * rows, (side + 1) * rows)
        cross = gram_a[mine, rows:roots] if side == 0 else gram_b[mine, :rows]
        parts = (gram_b[mine, mine], cross, gram_b[mine, knots:], gram_a[mine, mine], gram_a[mine, roots:])
        at = 0
        for part in parts:
            wide = part.shape[1]
            total[side, :, :, at : at + wide] = part.reshape(*total.shape[1:3], wide)
            at += wide
    core = core_ref[0]
    keep_ref[...] = total[core]
    send_ref[...] = total[1 - core]


def split3(x):
    high = x.astype(BF16)
    rest = x - high.astype(F32)
    mid = rest.astype(BF16)
    low = (rest - mid.astype(F32)).astype(BF16)
    return high, mid, low


def split_dot(left, right, dims, terms=6):
    lh, lm, ll = split3(left)
    rh, rm, rl = split3(right)
    lefts = jnp.concatenate([lh, lh, lm, lh, ll, lm][:terms], axis=dims[0])
    rights = jnp.concatenate([rh, rm, rh, rl, rh, rm][:terms], axis=dims[1])
    return lax.dot_general(
        lefts, rights, (((dims[0],), (dims[1],)), ((), ())), preferred_element_type=F32
    )


def factor_inverse(work, diag, panel):
    size = work.shape[0]
    tiles = size // 128

    def block(base, k, _):
        start = pl.multiple_of(k * STEP, STEP)
        corner = work[pl.ds(start, STEP), base : base + 128]
        diag[...] = pltpu.roll(corner, lax.rem(128 - (start - base), 128), 1)
        held = work[pl.ds(start, STEP), :]
        sub = lax.broadcasted_iota(jnp.int32, (8, 128), 0)
        at = sub * 128 + lax.broadcasted_iota(jnp.int32, (8, 128), 1) - start
        inside = (at >= 0) & (at < STEP)
        d, v = [], []
        for i in range(STEP):
            row = jnp.broadcast_to(diag[i : i + 1, :], (8, 128))
            d.append([None] * i + [jnp.broadcast_to(row[:, j : j + 1], (8, 128)) for j in range(i, STEP)])
            full = jnp.broadcast_to(held[i : i + 1, 0:128], (8, 128))
            for t in range(1, tiles):
                more = held[i : i + 1, t * 128 : (t + 1) * 128]
                full = jnp.where(sub == t, jnp.broadcast_to(more, (8, 128)), full)
            v.append(jnp.where(inside, jnp.where(at == i, 1.0, 0.0), full))
        for p in range(STEP):
            scale = lax.rsqrt(d[p][p])
            u = [None] * (p + 1) + [d[p][j] * scale for j in range(p + 1, STEP)]
            done = v[p] * scale
            panel[tiles * p : tiles * (p + 1), :] = done[0:tiles, :]
            for i in range(p + 1, STEP):
                for j in range(i, STEP):
                    d[i][j] = d[i][j] - u[i] * u[j]
                v[i] = v[i] - u[i] * done
        rows = jnp.concatenate(
            [panel[pl.ds(t, STEP, stride=tiles), :] for t in range(tiles)], axis=1
        )
        lane_p = lax.broadcasted_iota(jnp.int32, (STEP, size), 1)
        high, mid, low = split3(rows)
        later = lane_p >= start + STEP
        zero = jnp.zeros_like(high)
        th, tm, tl = (jnp.where(later, x, zero) for x in (high, mid, low))
        left = jnp.concatenate([th, th, tm, th, tl, tm], axis=0)
        right = jnp.concatenate([high, mid, high, low, high, mid], axis=0)
        change = rows_dot(left[:, base:], right)
        lane_a = lax.broadcasted_iota(jnp.int32, change.shape, 1)
        row_a = lax.broadcasted_iota(jnp.int32, change.shape, 0) + base
        fresh = (lane_a >= start) & (lane_a < start + STEP) & (row_a >= start + STEP)
        work[base:, :] = jnp.where(fresh, 0.0, work[base:, :]) - change
        work[pl.ds(start, STEP), :] = rows
        return 0

    for base in range(0, size, 128):
        lax.fori_loop(base // STEP, (base + 128) // STEP, functools.partial(block, base), 0)
    lane = lax.broadcasted_iota(jnp.int32, (size, size), 1)
    row = lax.broadcasted_iota(jnp.int32, (size, size), 0)
    return jnp.where(lane <= row, work[...], 0.0)


def factor_rows(matrix, first, inverse, scale):
    count = 8
    part = matrix[pl.ds(pl.multiple_of(first, 8), count), :]
    rows = split_dot(part, inverse, (1, 1), 3)
    lane = lax.broadcasted_iota(jnp.int32, rows.shape, 1)
    row = lax.broadcasted_iota(jnp.int32, rows.shape, 0) + first
    return jnp.where(lane <= row, rows, 0.0) * scale


def region_kernel(scale, leaf_ref, gathered_ref, column_ref, prior_ref,
                  solved_ref, schur_ref, factor_ref, matrix, work, diag, panel, half_ref):
    size = matrix.shape[0]
    first = leaf_ref[0] * 8
    width = size + solved_ref.shape[1]
    count = schur_ref.shape[0] * schur_ref.shape[1]
    core = lax.rem(leaf_ref[0], 2)
    mine = pl.multiple_of(core * count, count)
    lower = gathered_ref[count:, count:size]
    matrix[:count, :count] = gathered_ref[:count, :count]
    matrix[count:, count:] = gathered_ref[count:, :count]
    matrix[count:, :count] = lower
    matrix[:count, count:] = lower.T
    matrix[...] += prior_ref[0].astype(F32)
    work[...] = matrix[...]
    inverse = factor_inverse(work, diag, panel)
    half = split_dot(inverse, gathered_ref[:, size:width], (1, 0))
    half_ref[...] = half
    upper = gathered_ref[:count, count:size]
    near = column_ref[:, width : width + count]
    cross = jnp.where(core == 0, upper, upper.T)
    own = jnp.concatenate(
        [
            jnp.where(core == 0, near, cross),
            jnp.where(core == 0, cross, near),
            column_ref[:, width + count :],
        ],
        axis=1,
    )
    schur = own - split_dot(half_ref[:, pl.ds(mine, count)], half, (0, 0))
    schur_ref[...] = schur.reshape(schur_ref.shape)
    solved_ref[...] = split_dot(inverse, half, (0, 0), 3)
    factor_ref[0] = factor_rows(matrix, first, inverse, scale)


def root_kernel(scale, leaf_ref, summed_ref, prior_ref, solved_ref, knot_ref, pool_hbm, root_hbm,
                pred_ref, factor_ref, matrix, work, diag, panel, pool, root, sems):
    size = matrix.shape[0]
    loads = [
        pltpu.make_async_copy(pool_hbm.at[0], pool, sems.at[0]),
        pltpu.make_async_copy(root_hbm.at[0], root, sems.at[1]),
    ]
    for load in loads:
        load.start()
    first = leaf_ref[0] * 8
    matrix[...] = prior_ref[...].astype(F32) + summed_ref[:, :size]
    work[...] = matrix[...]
    inverse = factor_inverse(work, diag, panel)
    half = split_dot(inverse, summed_ref[:, size:], (1, 0), 3)
    root_coef = split_dot(inverse, half, (0, 0), 3)
    coef = solved_ref[:, size:] - split_dot(solved_ref[:, :size], root_coef, (1, 0), 3)
    knots = coef.shape[0]
    pick = one_hot(knot_ref[:, :knots], pool.shape[1])
    spread = jnp.dot(pick, coef.astype(BF16), preferred_element_type=F32).astype(BF16)
    factor_ref[...] = factor_rows(matrix, first, inverse, scale)
    for load in loads:
        load.wait()
    mean = jnp.dot(pool[...], spread, preferred_element_type=F32)
    mean = mean + jnp.dot(root[...], root_coef.astype(BF16), preferred_element_type=F32)
    pred_ref[0] = mean.astype(BF16)


VMEM = pl.BlockSpec(memory_space=pltpu.VMEM)
SMEM = pl.BlockSpec(memory_space=pltpu.SMEM)
ANY = pl.BlockSpec(memory_space=pl.ANY)


def per_device(
    leaf_factor, basis_pool, root_basis, responses, knot_order, region_prior, root_prior
):
    knots = region_prior.shape[1]
    roots = root_prior.shape[0]
    cols = responses.shape[2]
    leaf_count = lax.axis_size("leaf")
    region_count = lax.axis_size("region")
    chips = leaf_count // 2
    rows = leaf_factor.shape[2]
    pool = basis_pool.shape[2]
    leaf = lax.axis_index("leaf").astype(jnp.int32)
    leaf_at = leaf.reshape(1)
    core_at = lax.rem(leaf, 2).reshape(1)
    share = knots // leaf_count
    wide_b = knots + roots + cols
    wide_a = roots + cols

    def shape(*dims):
        return jax.ShapeDtypeStruct(dims, F32)

    width = wide_b + wide_a - knots // 2
    piece = shape(chips, share, width)
    keep, send = pl.pallas_call(
        grams_kernel,
        out_shape=(piece, piece),
        in_specs=[SMEM, VMEM, ANY, ANY, ANY, ANY],
        out_specs=(VMEM, VMEM),
        scratch_shapes=[
            pltpu.VMEM((rows, wide_b), BF16),
            pltpu.VMEM((rows, rows), BF16),
            pltpu.VMEM((rows, pool), BF16),
            pltpu.VMEM((2, chips, share, width), F32),
            pltpu.SemaphoreType.DMA((4,)),
        ],
        name="grams",
    )(core_at, knot_order, leaf_factor, basis_pool, root_basis, responses)

    swap = [(i, i ^ 1) for i in range(leaf_count)]
    same_core = [list(range(c, leaf_count, 2)) for c in range(2)]
    same_chip = [[i, i + 1] for i in range(0, leaf_count, 2)]
    paired = keep + lax.ppermute(send, "leaf", swap)
    arrived = lax.all_to_all(paired, "leaf", 0, 0, axis_index_groups=same_core, tiled=True)
    column = lax.all_gather(
        arrived.sum(axis=0), "leaf", axis=0, axis_index_groups=same_core, tiled=True
    )
    gathered = lax.all_gather(
        column[:, :wide_b], "leaf", axis=0, axis_index_groups=same_chip, tiled=True
    )

    square = pltpu.VMEM((knots, knots), F32)
    small = [pltpu.VMEM((STEP, 128), F32), pltpu.VMEM((STEP * knots // 128, 128), F32)]
    obs = rows * leaf_count
    chunk = roots // region_count // 2
    part = shape(region_count, chunk, wide_a)
    solved, schur, region_factor = pl.pallas_call(
        lambda *refs: region_kernel(1.0 / math.sqrt(obs), *refs),
        out_shape=(shape(knots, wide_a), part, shape(1, share, knots)),
        in_specs=[SMEM, VMEM, VMEM, VMEM],
        out_specs=(VMEM,) * 3,
        scratch_shapes=[square, square, *small, pltpu.VMEM((knots, wide_a), F32)],
        name="region_solve",
    )(leaf_at, gathered, column, region_prior)

    schur = lax.all_to_all(schur, "region", 0, 0, tiled=True)
    copies = jnp.broadcast_to(schur.sum(axis=0)[None], part.shape)
    summed = lax.all_to_all(copies, "region", 0, 0, tiled=True).reshape(roots // 2, wide_a)
    summed = lax.all_gather(summed, "leaf", axis=0, axis_index_groups=same_chip, tiled=True)

    predictions, root_factor = pl.pallas_call(
        lambda *refs: root_kernel(1.0 / math.sqrt(obs * region_count), *refs),
        out_shape=(
            jax.ShapeDtypeStruct((1, rows, cols), BF16),
            jax.ShapeDtypeStruct((share, roots), F32),
        ),
        in_specs=[SMEM, VMEM, VMEM, VMEM, VMEM, ANY, ANY],
        out_specs=(VMEM, VMEM),
        scratch_shapes=[
            square, square, *small,
            pltpu.VMEM((rows, pool), BF16),
            pltpu.VMEM((rows, roots), BF16),
            pltpu.SemaphoreType.DMA((2,)),
        ],
        name="root_solve",
    )(leaf_at, summed, root_prior, solved, knot_order, basis_pool, root_basis)
    return predictions, region_factor, root_factor


def solution(mesh):
    placed = (
        P("region", "leaf", None),
        P("region", "leaf", None),
        P("region", "leaf", None),
        P("region", "leaf", None),
        P("region", None),
        P("region", None, None),
        P(),
    )
    return jax.shard_map(
        per_device,
        mesh=mesh,
        in_specs=placed,
        out_specs=(P("region", "leaf", None), P("region", "leaf", None), P("leaf", None)),
        check_vma=False,
    )
```

```python
import functools
import math

import jax
import jax.numpy as jnp
from jax import lax
from jax.experimental import pallas as pl
from jax.experimental.pallas import tpu as pltpu
from jax.sharding import PartitionSpec as P

STEP = 16
HI = lax.Precision.HIGHEST
F32 = jnp.float32
BF16 = jnp.bfloat16


def rows_dot(left, right, precision=None):
    return lax.dot_general(
        left, right, (((0,), (0,)), ((), ())), precision=precision, preferred_element_type=F32
    )


def one_hot(knots, pool):
    count = knots.shape[1]
    ids = lax.broadcasted_iota(jnp.int32, (pool, count), 0)
    return (ids == knots).astype(BF16)


def grams_kernel(knot_ref, factor_hbm, pool_hbm, root_hbm, resp_hbm,
                 total, joined, factor, pool, sems):
    roots = root_hbm.shape[2]
    width = joined.shape[1]
    knots = width - roots - resp_hbm.shape[2]
    loads = [
        pltpu.make_async_copy(pool_hbm.at[0], pool, sems.at[0]),
        pltpu.make_async_copy(root_hbm.at[0], joined.at[:, pl.ds(knots, roots)], sems.at[1]),
        pltpu.make_async_copy(
            resp_hbm.at[0], joined.at[:, pl.ds(knots + roots, width - knots - roots)], sems.at[2]
        ),
        pltpu.make_async_copy(factor_hbm.at[0], factor, sems.at[3]),
    ]
    for load in loads:
        load.start()
    pick = one_hot(knot_ref[:, :knots], pool.shape[1])
    loads[0].wait()
    basis = jnp.dot(pool[...], pick, preferred_element_type=F32)
    joined[:, :knots] = basis.astype(BF16)
    for load in loads[1:]:
        load.wait()
    white = rows_dot(factor[...], joined[...]).astype(BF16)
    gram_b = rows_dot(white[:, :knots], white)
    gram_a = rows_dot(white[:, knots : knots + roots], white[:, knots:])
    rows = knots // 2
    for side in range(2):
        mine = slice(side * rows, (side + 1) * rows)
        cross = gram_a[mine, rows:roots] if side == 0 else gram_b[mine, :rows]
        parts = (gram_b[mine, mine], cross, gram_b[mine, knots:], gram_a[mine, mine], gram_a[mine, roots:])
        at = 0
        for part in parts:
            wide = part.shape[1]
            total[side, :, :, at : at + wide] = part.reshape(*total.shape[1:3], wide)
            at += wide


def split3(x):
    high = x.astype(BF16)
    rest = x - high.astype(F32)
    mid = rest.astype(BF16)
    low = (rest - mid.astype(F32)).astype(BF16)
    return high, mid, low


def split_dot(left, right, dims, terms=6):
    lh, lm, ll = split3(left)
    rh, rm, rl = split3(right)
    lefts = jnp.concatenate([lh, lh, lm, lh, ll, lm][:terms], axis=dims[0])
    rights = jnp.concatenate([rh, rm, rh, rl, rh, rm][:terms], axis=dims[1])
    return lax.dot_general(
        lefts, rights, (((dims[0],), (dims[1],)), ((), ())), preferred_element_type=F32
    )


def factor_inverse(work, diag, panel):
    size = work.shape[0]
    tiles = size // 128

    def block(base, k, _):
        start = pl.multiple_of(k * STEP, STEP)
        corner = work[pl.ds(start, STEP), base : base + 128]
        diag[...] = pltpu.roll(corner, lax.rem(128 - (start - base), 128), 1)
        held = work[pl.ds(start, STEP), :]
        sub = lax.broadcasted_iota(jnp.int32, (8, 128), 0)
        at = sub * 128 + lax.broadcasted_iota(jnp.int32, (8, 128), 1) - start
        inside = (at >= 0) & (at < STEP)
        d, v = [], []
        for i in range(STEP):
            row = jnp.broadcast_to(diag[i : i + 1, :], (8, 128))
            d.append([None] * i + [jnp.broadcast_to(row[:, j : j + 1], (8, 128)) for j in range(i, STEP)])
            full = jnp.broadcast_to(held[i : i + 1, 0:128], (8, 128))
            for t in range(1, tiles):
                more = held[i : i + 1, t * 128 : (t + 1) * 128]
                full = jnp.where(sub == t, jnp.broadcast_to(more, (8, 128)), full)
            v.append(jnp.where(inside, jnp.where(at == i, 1.0, 0.0), full))
        for p in range(STEP):
            scale = lax.rsqrt(d[p][p])
            u = [None] * (p + 1) + [d[p][j] * scale for j in range(p + 1, STEP)]
            done = v[p] * scale
            panel[tiles * p : tiles * (p + 1), :] = done[0:tiles, :]
            for i in range(p + 1, STEP):
                for j in range(i, STEP):
                    d[i][j] = d[i][j] - u[i] * u[j]
                v[i] = v[i] - u[i] * done
        rows = jnp.concatenate(
            [panel[pl.ds(t, STEP, stride=tiles), :] for t in range(tiles)], axis=1
        )
        lane_p = lax.broadcasted_iota(jnp.int32, (STEP, size), 1)
        high, mid, low = split3(rows)
        later = lane_p >= start + STEP
        zero = jnp.zeros_like(high)
        th, tm, tl = (jnp.where(later, x, zero) for x in (high, mid, low))
        left = jnp.concatenate([th, th, tm, th, tl, tm], axis=0)
        right = jnp.concatenate([high, mid, high, low, high, mid], axis=0)
        change = rows_dot(left[:, base:], right)
        lane_a = lax.broadcasted_iota(jnp.int32, change.shape, 1)
        row_a = lax.broadcasted_iota(jnp.int32, change.shape, 0) + base
        fresh = (lane_a >= start) & (lane_a < start + STEP) & (row_a >= start + STEP)
        work[base:, :] = jnp.where(fresh, 0.0, work[base:, :]) - change
        work[pl.ds(start, STEP), :] = rows
        return 0

    for base in range(0, size, 128):
        lax.fori_loop(base // STEP, (base + 128) // STEP, functools.partial(block, base), 0)
    lane = lax.broadcasted_iota(jnp.int32, (size, size), 1)
    row = lax.broadcasted_iota(jnp.int32, (size, size), 0)
    return jnp.where(lane <= row, work[...], 0.0)


def factor_rows(matrix, first, inverse, scale):
    count = 8
    part = matrix[pl.ds(pl.multiple_of(first, 8), count), :]
    rows = split_dot(part, inverse, (1, 1), 3)
    lane = lax.broadcasted_iota(jnp.int32, rows.shape, 1)
    row = lax.broadcasted_iota(jnp.int32, rows.shape, 0) + first
    return jnp.where(lane <= row, rows, 0.0) * scale


def region_kernel(scale, leaf_ref, gathered_ref, column_ref, prior_ref,
                  solved_ref, schur_ref, factor_ref, matrix, work, diag, panel, half_ref):
    size = matrix.shape[0]
    first = leaf_ref[0] * 8
    width = size + solved_ref.shape[1]
    count = schur_ref.shape[0] * schur_ref.shape[1]
    core = lax.rem(leaf_ref[0], 2)
    mine = pl.multiple_of(core * count, count)
    lower = gathered_ref[count:, count:size]
    matrix[:count, :count] = gathered_ref[:count, :count]
    matrix[count:, count:] = gathered_ref[count:, :count]
    matrix[count:, :count] = lower
    matrix[:count, count:] = lower.T
    matrix[...] += prior_ref[0].astype(F32)
    work[...] = matrix[...]
    inverse = factor_inverse(work, diag, panel)
    half = split_dot(inverse, gathered_ref[:, size:width], (1, 0))
    half_ref[...] = half
    upper = gathered_ref[:count, count:size]
    near = column_ref[:, width : width + count]
    cross = jnp.where(core == 0, upper, upper.T)
    own = jnp.concatenate(
        [
            jnp.where(core == 0, near, cross),
            jnp.where(core == 0, cross, near),
            column_ref[:, width + count :],
        ],
        axis=1,
    )
    schur = own - split_dot(half_ref[:, pl.ds(mine, count)], half, (0, 0))
    schur_ref[...] = schur.reshape(schur_ref.shape)
    solved_ref[...] = split_dot(inverse, half, (0, 0), 3)
    factor_ref[0] = factor_rows(matrix, first, inverse, scale)


def root_kernel(scale, leaf_ref, summed_ref, prior_ref, solved_ref, knot_ref, pool_hbm, root_hbm,
                pred_ref, factor_ref, matrix, work, diag, panel, pool, root, sems):
    size = matrix.shape[0]
    loads = [
        pltpu.make_async_copy(pool_hbm.at[0], pool, sems.at[0]),
        pltpu.make_async_copy(root_hbm.at[0], root, sems.at[1]),
    ]
    for load in loads:
        load.start()
    first = leaf_ref[0] * 8
    matrix[...] = prior_ref[...].astype(F32) + summed_ref[:, :size]
    work[...] = matrix[...]
    inverse = factor_inverse(work, diag, panel)
    half = split_dot(inverse, summed_ref[:, size:], (1, 0), 3)
    root_coef = split_dot(inverse, half, (0, 0), 3)
    coef = solved_ref[:, size:] - split_dot(solved_ref[:, :size], root_coef, (1, 0), 3)
    knots = coef.shape[0]
    pick = one_hot(knot_ref[:, :knots], pool.shape[1])
    spread = jnp.dot(pick, coef.astype(BF16), preferred_element_type=F32).astype(BF16)
    factor_ref[...] = factor_rows(matrix, first, inverse, scale)
    for load in loads:
        load.wait()
    mean = jnp.dot(pool[...], spread, preferred_element_type=F32)
    mean = mean + jnp.dot(root[...], root_coef.astype(BF16), preferred_element_type=F32)
    pred_ref[0] = mean.astype(BF16)


VMEM = pl.BlockSpec(memory_space=pltpu.VMEM)
SMEM = pl.BlockSpec(memory_space=pltpu.SMEM)
ANY = pl.BlockSpec(memory_space=pl.ANY)


def per_device(
    leaf_factor, basis_pool, root_basis, responses, knot_order, region_prior, root_prior
):
    knots = region_prior.shape[1]
    roots = root_prior.shape[0]
    cols = responses.shape[2]
    leaf_count = lax.axis_size("leaf")
    region_count = lax.axis_size("region")
    chips = leaf_count // 2
    rows = leaf_factor.shape[2]
    pool = basis_pool.shape[2]
    leaf = lax.axis_index("leaf").astype(jnp.int32)
    leaf_at = leaf.reshape(1)
    share = knots // leaf_count
    wide_b = knots + roots + cols
    wide_a = roots + cols

    def shape(*dims):
        return jax.ShapeDtypeStruct(dims, F32)

    width = wide_b + wide_a - knots // 2
    halves = pl.pallas_call(
        grams_kernel,
        out_shape=shape(2, chips, share, width),
        in_specs=[VMEM, ANY, ANY, ANY, ANY],
        out_specs=VMEM,
        scratch_shapes=[
            pltpu.VMEM((rows, wide_b), BF16),
            pltpu.VMEM((rows, rows), BF16),
            pltpu.VMEM((rows, pool), BF16),
            pltpu.SemaphoreType.DMA((4,)),
        ],
        name="grams",
    )(knot_order, leaf_factor, basis_pool, root_basis, responses)

    same_core = [list(range(c, leaf_count, 2)) for c in range(2)]
    same_chip = [[i, i + 1] for i in range(0, leaf_count, 2)]
    paired = lax.all_to_all(halves, "leaf", 0, 0, axis_index_groups=same_chip, tiled=True)
    paired = paired.sum(axis=0)
    arrived = lax.all_to_all(paired, "leaf", 0, 0, axis_index_groups=same_core, tiled=True)
    column = lax.all_gather(
        arrived.sum(axis=0), "leaf", axis=0, axis_index_groups=same_core, tiled=True
    )
    gathered = lax.all_gather(
        column[:, :wide_b], "leaf", axis=0, axis_index_groups=same_chip, tiled=True
    )

    square = pltpu.VMEM((knots, knots), F32)
    small = [pltpu.VMEM((STEP, 128), F32), pltpu.VMEM((STEP * knots // 128, 128), F32)]
    obs = rows * leaf_count
    chunk = roots // region_count // 2
    part = shape(region_count, chunk, wide_a)
    solved, schur, region_factor = pl.pallas_call(
        lambda *refs: region_kernel(1.0 / math.sqrt(obs), *refs),
        out_shape=(shape(knots, wide_a), part, shape(1, share, knots)),
        in_specs=[SMEM, VMEM, VMEM, VMEM],
        out_specs=(VMEM,) * 3,
        scratch_shapes=[square, square, *small, pltpu.VMEM((knots, wide_a), F32)],
        name="region_solve",
    )(leaf_at, gathered, column, region_prior)

    schur = lax.all_to_all(schur, "region", 0, 0, tiled=True)
    copies = jnp.broadcast_to(schur.sum(axis=0)[None], part.shape)
    summed = lax.all_to_all(copies, "region", 0, 0, tiled=True).reshape(roots // 2, wide_a)
    summed = lax.all_gather(summed, "leaf", axis=0, axis_index_groups=same_chip, tiled=True)

    predictions, root_factor = pl.pallas_call(
        lambda *refs: root_kernel(1.0 / math.sqrt(obs * region_count), *refs),
        out_shape=(
            jax.ShapeDtypeStruct((1, rows, cols), BF16),
            jax.ShapeDtypeStruct((share, roots), F32),
        ),
        in_specs=[SMEM, VMEM, VMEM, VMEM, VMEM, ANY, ANY],
        out_specs=(VMEM, VMEM),
        scratch_shapes=[
            square, square, *small,
            pltpu.VMEM((rows, pool), BF16),
            pltpu.VMEM((rows, roots), BF16),
            pltpu.SemaphoreType.DMA((2,)),
        ],
        name="root_solve",
    )(leaf_at, summed, root_prior, solved, knot_order, basis_pool, root_basis)
    return predictions, region_factor, root_factor


def solution(mesh):
    placed = (
        P("region", "leaf", None),
        P("region", "leaf", None),
        P("region", "leaf", None),
        P("region", "leaf", None),
        P("region", None),
        P("region", None, None),
        P(),
    )
    return jax.shard_map(
        per_device,
        mesh=mesh,
        in_specs=placed,
        out_specs=(P("region", "leaf", None), P("region", "leaf", None), P("leaf", None)),
        check_vma=False,
    )
```
